128 devices in a mesh: dp: 16 (over x, y_lo, core), mp: 8 (over y_hi, z).
Axes of the slice: x: 4, y: 4 (y_hi: 2, y_lo: 2; y = y_hi * 2 + y_lo), z: 4, core: 2. Of those that a mesh axis runs over, the one named last changes fastest.
Arguments:
- tokens: bfloat16 [32768, 1024], P(('dp', 'mp')), may hold values from -6 to 6
- cotangent: bfloat16 [32768, 1024], P(('dp', 'mp')), may hold values from -24 to 24
- weight_in: float32 [1024, 4096], P('dp', 'mp'), may hold values from -0.1875 to 0.1875
- weight_out: float32 [4096, 1024], P('mp', 'dp'), may hold values from -0.09375 to 0.09375
- moment_in: float32 [1024, 4096], P('dp', 'mp'), may hold values from -4 to 4
- second_in: float32 [1024, 4096], P('dp', 'mp'), may hold values from 0.01 to 1
- moment_out: float32 [4096, 1024], P('mp', 'dp'), may hold values from -4 to 4
- second_out: float32 [4096, 1024], P('mp', 'dp'), may hold values from 0.01 to 1
Outputs:
- input_grad: bfloat16 [32768, 1024], P(('dp', 'mp'))
- new_weight_in: float32 [1024, 4096], P('dp', 'mp')
- new_moment_in: float32 [1024, 4096], P('dp', 'mp')
- new_second_in: float32 [1024, 4096], P('dp', 'mp')
- new_weight_out: float32 [4096, 1024], P('mp', 'dp')
- new_moment_out: float32 [4096, 1024], P('mp', 'dp')
- new_second_out: float32 [4096, 1024], P('mp', 'dp')
The draws below stay inside these ranges and needn't reach their ends.
All inputs are finite; a program needn't handle non-finite values.
Results may differ from the reference program's by a relative error of at most 0.0071.
Values may be sent and summed in bfloat16 or wider, within the bound.
No kernel may reach another device: no remote copies, remote signals or barrier semaphores. Data moves between devices by JAX's collectives and lax.ppermute only.
A program may use at most 64 MiB of HBM per device.

```python
import math
import jax
import jax.numpy as jnp
from jax import lax

D = 1024
FF = 4096
TOK_DEV = 256
STEP = 1000
TOKENS = 32768
N_MP = 8


def raised(entries, key, source, target, parts, factor):
    owner, partner = [(jnp.arange(entries.shape[position]) // (entries.shape[position] // parts)).reshape([-1 if axis == position else 1 for axis in range(entries.ndim)]) for position in (source, target)]
    chosen = jax.random.permutation(key, parts)[partner]
    strong = (owner == chosen) | (owner == (partner + parts // 2) % parts)
    return jnp.where(strong, factor * entries, entries)


def levels(own_key, dims, shards, smallest, largest):
    factor_of = 1.0
    for axis_at, shards_of in shards:
        draws = jax.random.uniform(jax.random.fold_in(jax.random.fold_in(own_key, 6), axis_at), (shards_of,), jnp.float32, smallest / len(shards), largest / len(shards))
        factor_of = factor_of * jnp.repeat(jnp.exp(draws), dims[axis_at] // shards_of).reshape((-1,) + (1,) * (len(dims) - 1 - axis_at))
    return factor_of


def bell_draw(stream_key, extent, spread, reach, cuts=(), held_as=jnp.bfloat16):
    entries = spread * jax.random.normal(stream_key, extent, jnp.float32)
    if cuts:
        entries = entries * levels(stream_key, extent, cuts, -0.22, 0.18)
    return jnp.clip(entries, -reach, reach).astype(held_as)


def heavy_noise(stream_key, dims, deviation, bound, pieces, heavy, held_as=jnp.bfloat16):
    array = deviation * jax.random.normal(stream_key, dims, jnp.float32)
    if pieces:
        array = array * levels(stream_key, dims, pieces, -0.22, 0.18)
    return jnp.clip(raised(array, jax.random.fold_in(stream_key, 3), *heavy), -bound, bound).astype(held_as)


def setup_inputs(seed: int = 0) -> dict:
    streams_of = jax.random.split(jax.random.key(seed), 9)
    tokens = bell_draw(streams_of[0], (TOKENS, D), 1.0, 6.0, ((0, 128),))
    cotangent = heavy_noise(streams_of[1], (TOKENS, D), 1.0, 24.0, ((0, 128),), (0, 1, 128, 5.5))
    weight_in = bell_draw(streams_of[2], (D, FF), D ** -0.5, 0.1875, ((0, 16), (1, 8)), jnp.float32)
    weight_out = bell_draw(streams_of[3], (FF, D), FF ** -0.5, 0.09375, ((0, 8), (1, 16)), jnp.float32)
    moment_in = bell_draw(streams_of[4], (D, FF), 0.3, 4.0, ((0, 16), (1, 8)), jnp.float32)
    second_in = jnp.clip(jnp.exp(math.log(1.0) - 4.6051702 * jax.random.uniform(streams_of[5], (D, FF), jnp.float32) ** levels(streams_of[5], (D, FF), ((0, 16), (1, 8)), -0.2, 0.2)), 0.01, 1.0)
    moment_out = bell_draw(streams_of[6], (FF, D), 0.3, 4.0, ((0, 8), (1, 16)), jnp.float32)
    second_out = jnp.clip(jnp.exp(math.log(1.0) - 4.6051702 * jax.random.uniform(streams_of[7], (FF, D), jnp.float32) ** levels(streams_of[7], (FF, D), ((0, 8), (1, 16)), -0.2, 0.2)), 0.01, 1.0)
    return {"tokens": tokens, "cotangent": cotangent, "weight_in": weight_in, "weight_out": weight_out, "moment_in": moment_in, "second_in": second_in, "moment_out": moment_out, "second_out": second_out}


BETA_ONE = 0.9
BETA_TWO = 0.999
EPSILON = 1e-08
LEARN_RATE = 0.001
DECAY_RATE = 0.1

def normalize(rows):
    values = rows.astype(jnp.float32)
    inverse = lax.rsqrt(lax.optimization_barrier(jnp.mean(values * values, axis=-1, keepdims=True)) + 1e-06)
    return (values * inverse, inverse)

def activate(values):
    return jax.nn.gelu(values, approximate=True)

def adam_step(weight, moment, second, gradient):
    moment_new = BETA_ONE * moment + (1.0 - BETA_ONE) * gradient
    second_new = BETA_TWO * second + (1.0 - BETA_TWO) * gradient * gradient
    first_fix = 1.0 - BETA_ONE ** float(STEP)
    second_fix = 1.0 - BETA_TWO ** float(STEP)
    update = moment_new / first_fix / (jnp.sqrt(second_new / second_fix) + EPSILON)
    weight_new = weight - LEARN_RATE * (update + DECAY_RATE * weight)
    return (weight_new, moment_new, second_new)

def contract_rows(left, right):
    return lax.dot_general(left, right, (((0,), (0,)), ((), ())), preferred_element_type=jnp.float32)

def reference(tokens, cotangent, weight_in, weight_out, moment_in, second_in, moment_out, second_out):
    weight_in_b = weight_in.astype(jnp.bfloat16)
    weight_out_b = weight_out.astype(jnp.bfloat16)
    block = TOK_DEV * N_MP
    token_blocks = tokens.reshape(TOKENS // block, block, D)
    grad_blocks = cotangent.reshape(TOKENS // block, block, D)

    def visit(carry, pair):
        rows, upstream = pair
        normed_f, inverse = normalize(rows)
        normed = normed_f.astype(jnp.bfloat16)
        preact = jnp.dot(normed, weight_in_b, preferred_element_type=jnp.float32)
        activated, backward = jax.vjp(activate, preact)
        hidden = activated.astype(jnp.bfloat16)
        grad_out = carry[1] + contract_rows(hidden, upstream)
        d_hidden = lax.dot_general(upstream, weight_out_b, (((1,), (1,)), ((), ())), preferred_element_type=jnp.float32)
        d_preact = backward(d_hidden)[0].astype(jnp.bfloat16)
        grad_in = carry[0] + contract_rows(normed, d_preact)
        d_normed = lax.dot_general(d_preact, weight_in_b, (((1,), (1,)), ((), ())), preferred_element_type=jnp.float32)
        d_rows = inverse * (d_normed - normed_f * lax.optimization_barrier(jnp.mean(d_normed * normed_f, axis=-1, keepdims=True)))
        return ((grad_in, grad_out), d_rows.astype(jnp.bfloat16))
    start = (jnp.zeros((D, FF), jnp.float32), jnp.zeros((FF, D), jnp.float32))
    sums, input_blocks = lax.scan(visit, start, (token_blocks, grad_blocks))
    grad_scale = 1.0 / jnp.sqrt(jnp.float32(TOKENS))
    grad_in = sums[0] * grad_scale
    grad_out = sums[1] * grad_scale
    new_weight_in, new_moment_in, new_second_in = adam_step(weight_in, moment_in, second_in, grad_in)
    new_weight_out, new_moment_out, new_second_out = adam_step(weight_out, moment_out, second_out, grad_out)
    input_grad = input_blocks.reshape(TOKENS, D)
    return (input_grad, new_weight_in, new_moment_in, new_second_in, new_weight_out, new_moment_out, new_second_out)
```

```python
import jax
import jax.numpy as jnp
from jax import lax
from jax.sharding import Mesh, PartitionSpec as P

TOK_DEV = 256
STEP = 1000


BETA_ONE = 0.9
BETA_TWO = 0.999
EPSILON = 1e-08
LEARN_RATE = 0.001
DECAY_RATE = 0.1

AXES = ("x", "yl", "c", "yh", "z")
YAX = ("yl", "yh")


def normalize(rows):
    values = rows.astype(jnp.float32)
    inverse = lax.rsqrt(jnp.mean(values * values, axis=-1, keepdims=True) + 1e-06)
    return (values * inverse, inverse)


def activate(values):
    return jax.nn.gelu(values, approximate=True)


def adam_step(weight, moment, second, gradient):
    moment_new = BETA_ONE * moment + (1.0 - BETA_ONE) * gradient
    second_new = BETA_TWO * second + (1.0 - BETA_TWO) * gradient * gradient
    first_fix = 1.0 - BETA_ONE ** float(STEP)
    second_fix = 1.0 - BETA_TWO ** float(STEP)
    update = moment_new / first_fix / (jnp.sqrt(second_new / second_fix) + EPSILON)
    weight_new = weight - LEARN_RATE * (update + DECAY_RATE * weight)
    return (weight_new, moment_new, second_new)


def contract_rows(left, right):
    return lax.dot_general(
        left, right, (((0,), (0,)), ((), ())), preferred_element_type=jnp.float32
    )


def y_slot(y):
    return (y % 2) * 2 + y // 2


def fetch(value, axis, offset):
    if axis == "y":
        pairs = [(y_slot((i + offset) % 4), y_slot(i)) for i in range(4)]
        return lax.ppermute(value, YAX, pairs)
    size = 2 if axis == "c" else 4
    return lax.ppermute(value, axis, [((i + offset) % size, i) for i in range(size)])


def gather_ring(value, axis):
    return jnp.stack([value] + [fetch(value, axis, k) for k in (1, 2, 3)])


def scatter_ring(parts, axis):
    total = parts[0].astype(jnp.float32)
    for k in (1, 2, 3):
        total = total + fetch(parts[k], axis, -k).astype(jnp.float32)
    return total


def shards(tokens, cotangent, weight_in, weight_out, moment_in, second_in, moment_out, second_out):
    x = lax.axis_index("x")
    y = lax.axis_index("yh") * 2 + lax.axis_index("yl")
    core = lax.axis_index("c")

    tok_p, tok_m = fetch(tokens, "z", 1), fetch(tokens, "z", -1)
    shard_in = weight_in.astype(jnp.bfloat16)
    shard_out = weight_out.T.astype(jnp.bfloat16)
    shard_in, shard_out = lax.optimization_barrier((shard_in, shard_out))
    half_in = gather_ring(shard_in, "x")
    half_out = gather_ring(shard_out, "y")
    cot_p, cot_m = fetch(cotangent, "z", 1), fetch(cotangent, "z", -1)
    whole_in = gather_ring(half_in, "y")
    whole_out = gather_ring(half_out, "x")
    tok_2 = jnp.concatenate([fetch(tok_p[:128], "z", 1), fetch(tok_m[128:], "z", -1)])
    cot_2 = jnp.concatenate([fetch(cot_p[:128], "z", 1), fetch(cot_m[128:], "z", -1)])

    def arrange(block):
        other = fetch(block, "c", 1)
        both = jnp.where(core == 0, jnp.stack([block, other]), jnp.stack([other, block]))
        both = jnp.roll(jnp.roll(both, y, axis=1), x, axis=2)
        both = both.reshape(2, 2, 2, 4, 64, 512)
        return both.transpose(3, 2, 0, 4, 1, 5).reshape(1024, 1024)

    weight_in_b = arrange(whole_in)
    weight_out_t = arrange(jnp.swapaxes(whole_out, 0, 1))

    def visit(rows, upstream):
        normed_f, inverse = normalize(rows)
        normed = normed_f.astype(jnp.bfloat16)
        preact = jnp.dot(normed, weight_in_b, preferred_element_type=jnp.float32)
        activated, backward = jax.vjp(activate, preact)
        hidden = activated.astype(jnp.bfloat16)
        d_hidden = jnp.dot(upstream, weight_out_t, preferred_element_type=jnp.float32)
        d_preact = backward(d_hidden)[0].astype(jnp.bfloat16)
        return normed, hidden, d_preact

    rows = jnp.concatenate([tokens, tok_p, tok_2, tok_m])
    upstream = jnp.concatenate([cotangent, cot_p, cot_2, cot_m])
    normed, hidden, d_preact = visit(rows, upstream)
    in_partial = contract_rows(normed, d_preact)
    out_partial = contract_rows(upstream, hidden)

    def reduce_grad(partial, first, second):
        parts = partial.astype(jnp.bfloat16).reshape(4, 2, 2, 64, 2, 512)
        parts = parts.transpose(2, 4, 1, 0, 3, 5).reshape(2, 4, 4, 64, 512)
        mine = jnp.where(core == 0, parts[0], parts[1])
        theirs = jnp.where(core == 0, parts[1], parts[0])
        summed = mine.astype(jnp.float32) + fetch(theirs, "c", 1).astype(jnp.float32)
        summed = jnp.roll(jnp.roll(summed.astype(jnp.bfloat16), -y, axis=0), -x, axis=1)
        if first == "x":
            summed = jnp.swapaxes(summed, 0, 1)
        summed = scatter_ring(summed, first).astype(jnp.bfloat16)
        return scatter_ring(summed, second)

    in_summed = reduce_grad(in_partial, "x", "y")
    out_summed = reduce_grad(out_partial, "y", "x").T
    d_part = lax.dot_general(
        d_preact, weight_in_b, (((1,), (1,)), ((), ())), preferred_element_type=jnp.float32
    )
    d_normed = d_part[:256]
    for k in (1, 2, 3):
        piece = d_part[256 * k : 256 * (k + 1)].astype(jnp.bfloat16)
        d_normed = d_normed + fetch(piece, "z", -k).astype(jnp.float32)
    normed_f, inverse = normalize(tokens)
    d_rows = inverse * (d_normed - normed_f * jnp.mean(d_normed * normed_f, axis=-1, keepdims=True))
    input_grad = d_rows.astype(jnp.bfloat16)
    token_count = TOK_DEV * 128
    grad_scale = 1.0 / jnp.sqrt(jnp.float32(token_count))
    new_weight_in, new_moment_in, new_second_in = adam_step(
        weight_in, moment_in, second_in, in_summed * grad_scale
    )
    new_weight_out, new_moment_out, new_second_out = adam_step(
        weight_out, moment_out, second_out, out_summed * grad_scale
    )
    return (
        input_grad,
        new_weight_in,
        new_moment_in,
        new_second_in,
        new_weight_out,
        new_moment_out,
        new_second_out,
    )


def solution(mesh):
    split = Mesh(mesh.devices.reshape(4, 2, 2, 2, 4), AXES)
    dp, mp = ("x", "yl", "c"), ("yh", "z")
    rows = P(AXES, None)
    w_in, w_out = P(dp, mp), P(mp, dp)
    return jax.shard_map(
        shards,
        mesh=split,
        in_specs=(rows, rows, w_in, w_out, w_in, w_in, w_out, w_out),
        out_specs=(rows, w_in, w_in, w_in, w_out, w_out, w_out),
        check_vma=False,
    )
```
